32 devices in a mesh: chan: 8 (over z, x), bl: 4 (over y, core).
Axes of the slice: x: 2, y: 2, z: 4, core: 2. Of those that a mesh axis runs over, the one named last changes fastest.
Arguments:
- visibilities: bfloat16 [1024, 1536, 2, 128], P('bl', 'chan'), may hold values from -6 to 6
- kernels: bfloat16 [64, 128, 256], replicated, may hold values from -0.1875 to 0.1875
- block_ids: int32 [4, 64, 8], P('bl'), may hold values from 0 to 255
- kernel_ids: int32 [4, 64, 8], P('bl'), may hold values from 0 to 63
- tile_counts: int32 [4, 64], P('bl'), may hold values from 1 to 8, as said below
- wedge_mask: int32 [64, 1536], P(('chan', 'bl')), may hold values 0 or 1
Outputs:
- delay_tiles: float32 [64, 2, 256, 1536], P(('chan', 'bl'))
The draws below stay inside these ranges and needn't reach their ends.
Inputs may be any that keep to these rules, and one draw needn't show every extreme that they name: `tile_counts`: slots at or past a tile's count are ignored; in every group some tile uses all 8 slots.
All inputs are finite; a program needn't handle non-finite values. No bound on the sum of `wedge_mask` on one device may be relied on, other than what follows from the above.
Results may differ from the reference program's by a relative error of at most 0.0095.
Values may be sent and summed in bfloat16 or wider, within the bound.
No kernel may reach another device: no remote copies, remote signals or barrier semaphores. Data moves between devices by JAX's collectives and lax.ppermute only.
A program may use at most 192 MiB of HBM per device.

```python
import math
import jax
import jax.numpy as jnp
from jax import lax

NCH = 1536
CELLS = 256
SB = 128
MOST = 8
NK = 64
NB = 256
TILES = 64
N_BL = 4


def draw_tile_counts(key, part):
    counts = jax.random.randint(key, (N_BL, TILES), 1, MOST + 1, dtype=jnp.int32)
    return counts.at[:, 0].set(MOST)


def with_ends(result, stream_key, least, top_value):
    place = [jax.random.randint(jax.random.fold_in(stream_key, axis), (), 0, length) for axis, length in enumerate(result.shape)]
    longest = result.shape.index(max(result.shape))
    neighbour = place[:longest] + [(place[longest] + 1) % result.shape[longest]] + place[longest + 1:]
    return result.at[tuple(place)].set(least).at[tuple(neighbour)].set(top_value)


def level_of(stream_key, shape, pieces, low, top_value):
    def one(position, blocks):
        heights = jax.random.uniform(jax.random.fold_in(jax.random.fold_in(stream_key, 6), position), (blocks,), jnp.float32, low / len(pieces), top_value / len(pieces))
        return jnp.repeat(jnp.exp(heights), shape[position] // blocks).reshape((-1,) + (1,) * (len(shape) - position - 1))

    loudness = one(*pieces[0])
    for cut in pieces[1:]:
        loudness = loudness * one(*cut)
    return loudness


def noise(key, dims, scale, reach, shards=(), held_as=jnp.bfloat16):
    level = level_of(key, dims, shards, -0.22, 0.18) if shards else 1.0
    array = jax.random.normal(key, dims, jnp.float32) * scale * level
    return jnp.minimum(jnp.maximum(array, -reach), reach).astype(held_as)


def setup_inputs(seed: int = 0) -> dict:
    key_of = jax.random.split(jax.random.key(seed), 7)
    visibilities = noise(key_of[0], (N_BL * NB, NCH, 2, SB), 1.0, 6.0, ((0, 4), (1, 8)))
    kernels = noise(key_of[1], (NK, SB, CELLS), (SB * MOST) ** -0.5, 0.1875)
    block_ids = with_ends(jax.random.randint(key_of[2], (N_BL, TILES, MOST), 0, NB), jax.random.fold_in(key_of[2], 1), 0, NB - 1).astype(jnp.int32)
    kernel_ids = with_ends(jax.random.randint(key_of[3], (N_BL, TILES, MOST), 0, NK), jax.random.fold_in(key_of[3], 1), 0, NK - 1).astype(jnp.int32)
    tile_counts = draw_tile_counts(jax.random.fold_in(key_of[6], 71), 0)
    wedge_mask = with_ends((jax.random.randint(key_of[5], (TILES, NCH), 0, 2) < 1).astype(jnp.int32), jax.random.fold_in(key_of[5], 1), 0, 1)
    return {"visibilities": visibilities, "kernels": kernels, "block_ids": block_ids, "kernel_ids": kernel_ids, "tile_counts": tile_counts, "wedge_mask": wedge_mask}


def delay_tables():
    chans = jnp.arange(NCH, dtype=jnp.int32)
    phase = chans[:, None] * chans[None, :] % NCH
    angle = phase.astype(jnp.float32) * (2.0 * math.pi / NCH)
    return (jnp.cos(angle).astype(jnp.bfloat16), jnp.sin(angle).astype(jnp.bfloat16))

def reference(visibilities, kernels, block_ids, kernel_ids, tile_counts, wedge_mask):
    blocked = visibilities.reshape(N_BL, NB, NCH, 2, SB)
    cosine, sine = delay_tables()
    slots = jnp.arange(MOST, dtype=jnp.int32)
    scale = 1.0 / math.sqrt(NCH)

    def one_tile(tile):
        total = jnp.zeros((NCH, 2, CELLS), jnp.float32)
        for group in range(N_BL):
            chosen = blocked[group][block_ids[group, tile]]
            keep = (slots < tile_counts[group, tile]).astype(jnp.bfloat16)
            weights = kernels[kernel_ids[group, tile]] * keep[:, None, None]
            part = jnp.einsum('kcps,ksx->cpx', chosen.astype(jnp.float32), weights.astype(jnp.float32))
            rounded = lax.optimization_barrier(part.astype(jnp.bfloat16))
            total = total + rounded.astype(jnp.float32)
        gridded = total.astype(jnp.bfloat16)
        real_part = gridded[:, 0].T
        imag_part = gridded[:, 1].T
        out_real = jnp.dot(real_part, cosine, preferred_element_type=jnp.float32) + jnp.dot(imag_part, sine, preferred_element_type=jnp.float32)
        out_imag = jnp.dot(imag_part, cosine, preferred_element_type=jnp.float32) - jnp.dot(real_part, sine, preferred_element_type=jnp.float32)
        keep_bins = wedge_mask[tile].astype(jnp.float32)
        return jnp.stack([out_real, out_imag]) * scale * keep_bins[None, None, :]
    return lax.map(one_tile, jnp.arange(TILES, dtype=jnp.int32))
```

```python
import functools
import math

import jax
import jax.numpy as jnp
import numpy as np
from jax import lax
from jax.experimental import pallas as pl
from jax.experimental.pallas import tpu as pltpu
from jax.sharding import PartitionSpec as P


UNIT = 16
SHARES = (1, 1)
DIRECT = (True, True, True, True)
PER = 2
RADIX = 4
LANES = 128


def piece_channels(ch_dev):
    units = ch_dev // UNIT
    ends = [round(units * sum(SHARES[: i + 1]) / sum(SHARES)) for i in range(len(SHARES))]
    return [(b - a) * UNIT for a, b in zip([0] + ends[:-1], ends)]


def after(x, *before):
    return lax.optimization_barrier((x,) + before)[0]


def xor_pairs(n, bit):
    return [(i, i ^ bit) for i in range(n)]


def grid_kernel(inner, owned, n_bl, off, flip, depth, lists_ref, vis, ker, out_ref):
    n_chan, rows = out_ref.shape[1:3]
    per = math.gcd(PER, n_chan)
    blocks = n_chan // per

    def step(g, _):
        half = g // blocks
        owner = lists_ref[2 * depth + 1, 0] ^ jnp.where(half == 0, 2, 0) ^ flip
        for i in range(per):
            chan = (g % blocks) * per + i
            tile = (chan * n_bl + owner) * owned + inner
            count = lists_ref[2 * depth, tile]
            lhs = [vis[lists_ref[k, tile], pl.ds(off, rows)] for k in range(depth)]
            lhs = [jnp.where(k < count, v, jnp.zeros_like(v)) for k, v in enumerate(lhs)]
            rhs = [ker[lists_ref[depth + k, tile]] for k in range(depth)]
            acc = jnp.dot(
                jnp.concatenate(lhs, axis=1), jnp.concatenate(rhs, axis=0), preferred_element_type=jnp.float32
            )
            out_ref[half, chan] = acc.astype(jnp.bfloat16)
        return 0

    lax.fori_loop(0, 2 * blocks, step, 0)


def grid_call(lists, vis, ker, inner, off, ch, n_chan, n_bl, owned, flip):
    vmem = pl.BlockSpec(memory_space=pltpu.VMEM)
    smem = pl.BlockSpec(memory_space=pltpu.SMEM)
    return pl.pallas_call(
        functools.partial(grid_kernel, inner, owned, n_bl, 2 * off, flip, (lists.shape[0] - 2) // 2),
        in_specs=[smem] + [vmem] * 2,
        out_specs=vmem,
        out_shape=jax.ShapeDtypeStruct((2, n_chan, 2 * ch, ker.shape[2]), jnp.bfloat16),
        compiler_params=pltpu.CompilerParams(vmem_limit_bytes=4 << 20),
    )(lists, vis, ker)


def pair_up(a, b):
    return (a.astype(jnp.float32) + b.astype(jnp.float32)).astype(jnp.bfloat16)


def sum_all(*parts):
    total = parts[0].astype(jnp.float32)
    for part in parts[1:]:
        total = total + part.astype(jnp.float32)
    return total.astype(jnp.bfloat16)


def sum_kernel(me_ref, keep_ref, near_ref, far_ref, *outs):
    for r, out in enumerate(outs):
        chan = me_ref[1] ^ r
        out[...] = sum_all(keep_ref[0, chan], near_ref[0, chan], far_ref[chan])


def sum_call(me, keep, near, far):
    _, n_chan, rows, cells = keep.shape
    half = pl.BlockSpec((1, n_chan, rows, cells), lambda i, *_: (1, 0, 0, 0))
    return pl.pallas_call(
        sum_kernel,
        grid_spec=pltpu.PrefetchScalarGridSpec(
            num_scalar_prefetch=1,
            grid=(1,),
            in_specs=[half, half, pl.BlockSpec((n_chan, rows, cells), lambda i, *_: (0, 0, 0))],
            out_specs=[pl.BlockSpec((rows, cells), lambda i, *_: (0, 0))] * n_chan,
        ),
        out_shape=[jax.ShapeDtypeStruct((rows, cells), jnp.bfloat16)] * n_chan,
        compiler_params=pltpu.CompilerParams(dimension_semantics=("arbitrary",), vmem_limit_bytes=12 << 20),
    )(me, keep, near, far)


def angle_tables(n_chan, ch_dev):
    nchan = n_chan * ch_dev
    delay = np.arange(nchan // RADIX, dtype=np.int64)
    start = np.arange(n_chan, dtype=np.int64)[:, None] * ch_dev
    inside = np.arange(ch_dev, dtype=np.int64).reshape(ch_dev // RADIX, RADIX).T[:, :, None]
    turn = lambda c: 2.0 * np.pi * (c * delay % nchan) / nchan
    return [jnp.asarray(f(turn(c)).astype(np.float32)) for c in (start, inside) for f in (np.cos, np.sin)]


def table_kernel(places, uc_ref, us_ref, vc_ref, vs_ref, *rest):
    n = len(places)
    outs, scratch = rest[:n], rest[n:]
    n_src = uc_ref.shape[0]
    for j, (off, ch) in enumerate(places):
        q = ch // RADIX
        cos, sin = scratch[2 * j], scratch[2 * j + 1]
        for m in range(RADIX):
            vc = vc_ref[m, pl.ds(off // RADIX, q), :]
            vs = vs_ref[m, pl.ds(off // RADIX, q), :]
            for r in range(n_src):
                uc = uc_ref[pl.ds(r, 1), :]
                us = us_ref[pl.ds(r, 1), :]
                cos[pl.ds(r * q, q), :] = uc * vc - us * vs
                sin[pl.ds(r * q, q), :] = us * vc + uc * vs
            k = n_src * q
            c = cos[...]
            s = sin[...]
            outs[j][0, m, pl.ds(0, k), pl.ds(0, LANES)] = c.astype(jnp.bfloat16)
            outs[j][0, m, pl.ds(0, k), pl.ds(LANES, LANES)] = (-s).astype(jnp.bfloat16)
            outs[j][0, m, pl.ds(k, k), pl.ds(0, LANES)] = s.astype(jnp.bfloat16)
            outs[j][0, m, pl.ds(k, k), pl.ds(LANES, LANES)] = c.astype(jnp.bfloat16)


def table_call(gate, sizes, n_chan, ch_dev):
    tables = angle_tables(n_chan, ch_dev)
    tables[0] = after(tables[0], gate)
    steps = tables[0].shape[-1] // LANES
    places, off = [], 0
    for ch in sizes:
        places.append((off, ch))
        off += ch
    spec = lambda t: pl.BlockSpec(t.shape[:-1] + (LANES,), lambda d, *_: (0,) * (t.ndim - 1) + (d,))
    return pl.pallas_call(
        functools.partial(table_kernel, places),
        grid=(steps,),
        in_specs=[spec(t) for t in tables],
        out_specs=[
            pl.BlockSpec((1, RADIX, 2 * n_chan * ch // RADIX, 2 * LANES), lambda d: (d, 0, 0, 0)) for ch in sizes
        ],
        scratch_shapes=[
            pltpu.VMEM((n_chan * ch // RADIX, LANES), jnp.float32) for ch in sizes for _ in range(2)
        ],
        out_shape=[
            jax.ShapeDtypeStruct((steps, RADIX, 2 * n_chan * ch // RADIX, 2 * LANES), jnp.bfloat16)
            for ch in sizes
        ],
        compiler_params=pltpu.CompilerParams(dimension_semantics=("arbitrary",), vmem_limit_bytes=12 << 20),
        name="tables",
    )(*tables)


def turn_kernel(counts, has_acc, inner, scale, me_ref, *refs):
    final = inner is not None
    rest = list(refs)
    gs = [[rest.pop(0) for _ in range(c)] for c in counts]
    ts = [rest.pop(0) for _ in counts]
    acc_ref = rest.pop(0) if has_acc else None
    if final:
        mask_ref, _, out_hbm, turned, stage, bins, sems = rest
    else:
        out_ref, turned, stage = rest
    d = pl.program_id(0)
    steps = pl.num_programs(0)

    @pl.when(d == 0)
    def _():
        at = 0
        for g in gs:
            if len(g) == 1:
                n_src, rows, _ = g[0].shape
            else:
                n_src, rows = len(g), g[0].shape[0]
            for r in range(n_src):
                for h in range(stage.shape[0]):
                    lanes = pl.ds(h * LANES, LANES)
                    if len(g) == 1:
                        stage[h, pl.ds(r * rows, rows), :] = g[0][r, :, lanes].astype(jnp.float32)
                    else:
                        start = pl.multiple_of((me_ref[1] ^ r) * rows, 8)
                        stage[h, pl.ds(start, rows), :] = g[r][:, lanes].astype(jnp.float32)
            k = n_src * rows // (2 * RADIX)
            for m in range(RADIX):
                for h in range(stage.shape[0]):
                    parts = [
                        stage[h, pl.ds(2 * m + p, k, stride=2 * RADIX), :].astype(jnp.bfloat16) for p in range(2)
                    ]
                    turned[m, pl.ds(h * LANES, LANES), pl.ds(at, 2 * k)] = jnp.concatenate(parts, axis=0).T
            at += 2 * k

    sums = []
    for m in range(RADIX):
        at = 0
        total = None
        for t in ts:
            k = t.shape[2]
            part = jnp.dot(turned[m, :, pl.ds(at, k)], t[0, m], preferred_element_type=jnp.float32)
            total = part if total is None else total + part
            at += k
        if has_acc:
            total = total + acc_ref[0, m]
        sums.append(total)
    if not final:
        for m in range(RADIX):
            out_ref[0, m] = sums[m]
        return

    def copies(step):
        slot = step % 2
        width = steps * LANES
        return [
            pltpu.make_async_copy(
                bins.at[slot, j],
                out_hbm.at[inner, :, :, pl.ds(pl.multiple_of(j * width + step * LANES, LANES), LANES)],
                sems.at[slot, j],
            )
            for j in range(RADIX)
        ]

    @pl.when(d >= 2)
    def _():
        for c in copies(d - 2):
            c.wait()

    re = [s[:, :LANES] for s in sums]
    im = [s[:, LANES:] for s in sums]
    e0r, e0i, e1r, e1i = re[0] + re[2], im[0] + im[2], re[0] - re[2], im[0] - im[2]
    o0r, o0i, o1r, o1i = re[1] + re[3], im[1] + im[3], re[1] - re[3], im[1] - im[3]
    joined = (
        (e0r + o0r, e0i + o0i),
        (e1r + o1i, e1i - o1r),
        (e0r - o0r, e0i - o0i),
        (e1r - o1i, e1i + o1r),
    )
    slot = d % 2
    for j, parts in enumerate(joined):
        at = pl.ds(pl.multiple_of((j * steps + d) * LANES, LANES), LANES)
        keep = mask_ref[pl.ds(inner, 1), at].astype(jnp.float32) * scale
        for p, value in enumerate(parts):
            bins[slot, j, p] = value * keep
    for c in copies(d):
        c.start()

    @pl.when(d == steps - 1)
    def _():
        for back in range(min(2, out_hbm.shape[3] // (RADIX * LANES)) - 1, -1, -1):
            for c in copies(d - back):
                c.wait()


def turn_call(me, gs, ts, acc, mask, out, inner):
    cells = gs[0][0].shape[-1]
    steps = ts[0].shape[0]
    final = inner is not None
    has_acc = acc is not None
    k = sum(t.shape[2] for t in ts)
    whole = lambda a: pl.BlockSpec(a.shape, lambda d, *_: (0,) * a.ndim, pipeline_mode=pl.Buffered(1))
    acc_spec = pl.BlockSpec((1, RADIX, cells, 2 * LANES), lambda d, *_: (d, 0, 0, 0))
    ins = [a for g in gs for a in g]
    specs = [whole(a) for a in ins]
    ins += ts
    specs += [pl.BlockSpec((1,) + t.shape[1:], lambda d, *_: (d, 0, 0, 0)) for t in ts]
    if has_acc:
        ins.append(acc)
        specs.append(acc_spec)
    scratch = [
        pltpu.VMEM((RADIX, cells, k), jnp.bfloat16),
        pltpu.VMEM((cells // LANES, max(sum(a.size for a in g) for g in gs) // cells, LANES), jnp.float32),
    ]
    if final:
        alias = {len(ins) + 2: 0}
        ins += [mask, out]
        specs += [whole(mask), pl.BlockSpec(memory_space=pltpu.HBM)]
        out_spec = pl.BlockSpec(memory_space=pltpu.HBM)
        out_shape = jax.ShapeDtypeStruct(out.shape, out.dtype)
        scratch += [
            pltpu.VMEM((2, RADIX, 2, cells, LANES), jnp.float32),
            pltpu.SemaphoreType.DMA((2, RADIX)),
        ]
    else:
        alias = {}
        out_spec = acc_spec
        out_shape = jax.ShapeDtypeStruct((steps, RADIX, cells, 2 * LANES), jnp.float32)
    nchan = steps * RADIX * LANES
    return pl.pallas_call(
        functools.partial(turn_kernel, [len(g) for g in gs], has_acc, inner, 1.0 / math.sqrt(nchan)),
        grid_spec=pltpu.PrefetchScalarGridSpec(
            num_scalar_prefetch=1,
            grid=(steps,),
            in_specs=specs,
            out_specs=out_spec,
            scratch_shapes=scratch,
        ),
        out_shape=out_shape,
        input_output_aliases=alias,
        compiler_params=pltpu.CompilerParams(dimension_semantics=("arbitrary",), vmem_limit_bytes=14 << 20),
    )(me, *ins)


def empty_kernel(out_ref):
    pass


def empty(shape):
    return pl.pallas_call(
        empty_kernel,
        out_specs=pl.BlockSpec(memory_space=pltpu.HBM),
        out_shape=jax.ShapeDtypeStruct(shape, jnp.float32),
        compiler_params=pltpu.CompilerParams(vmem_limit_bytes=1 << 20),
        name="empty",
    )()


def local(visibilities, kernels, block_ids, kernel_ids, tile_counts, wedge_mask):
    n_chan = lax.axis_size("chan")
    n_bl = lax.axis_size("bl")
    nblocks, ch_dev, _, block_len = visibilities.shape
    cells = kernels.shape[2]
    owned = wedge_mask.shape[0]
    nchan = ch_dev * n_chan
    vis = visibilities.reshape(nblocks, ch_dev * 2, block_len)
    me = jnp.stack([lax.axis_index("bl"), lax.axis_index("chan")]).astype(jnp.int32)
    place = jnp.full((1, tile_counts.shape[1]), me[0], jnp.int32)
    lists = jnp.concatenate([block_ids[0].T, kernel_ids[0].T, tile_counts, place], axis=0)
    sizes = piece_channels(ch_dev)
    n = len(sizes)
    starts = [sum(sizes[:j]) for j in range(n)]
    blocks = []
    for inner in range(owned):
        blocks += [(inner, j) for j in (range(n) if inner < owned - 1 else range(n - 1, -1, -1))]
    keep, near, sent, far, total, arrived = {}, {}, {}, {}, {}, {}
    tables = out = acc = None
    gate = me

    for what, i in order_of_work(len(blocks)):
        if what in ("give", "grid"):
            inner, j = blocks[i]
            part = grid_call(
                after(lists, gate), vis, kernels,
                inner, starts[j], sizes[j], n_chan, n_bl, owned, int(what == "give"),
            )
            gate = part
            if what == "grid":
                keep[i] = part
            else:
                near[i] = lax.ppermute(part, "bl", xor_pairs(n_bl, 1))
        elif what == "tables":
            tables = table_call(gate, sizes, n_chan, ch_dev)
            gate = tables[0]
        elif what == "pair":
            gate = sent[i] = pair_up(after(keep[i], gate)[0], near[i][0])
            far[i] = lax.ppermute(sent[i], "bl", xor_pairs(n_bl, 2))
        elif what == "sum":
            if DIRECT[i % len(DIRECT)]:
                total[i] = sum_call(me, after(keep[i], gate), near[i], far[i])
                gate = total[i][0]
            else:
                gate = total[i] = sum_all(after(keep[i], gate)[1], near[i][1], far[i])
        elif what == "spread":
            if DIRECT[i % len(DIRECT)]:
                arrived[blocks[i]] = [total[i][0]] + [
                    lax.ppermute(total[i][r], "chan", xor_pairs(n_chan, r)) for r in range(1, n_chan)
                ]
            else:
                arrived[blocks[i]] = [lax.all_to_all(total[i], "chan", 0, 0, tiled=True)]
        elif what == "join":
            if out is None:
                out = empty((owned, 2, cells, nchan))
            if i < owned - 1:
                got, last = [(i, j) for j in range(n)], True
            elif n > 1 and i == owned - 1:
                got, last = blocks[-n:-1], False
            else:
                got, last = blocks[-1:], True
            gs = [arrived[key] for key in got]
            gs[0] = [after(gs[0][0], gate)] + gs[0][1:]
            ts = [tables[j] for _, j in got]
            if last:
                gate = out = turn_call(me, gs, ts, acc, wedge_mask, out, got[0][0])
            else:
                gate = acc = turn_call(me, gs, ts, None, None, None, None)
    return out


ORDER = (
    ("give", 0), ("grid", 0), ("pair", 0), ("give", 1), ("grid", 1), ("give", 2), ("pair", 1), ("grid", 2),
    ("pair", 2), ("sum", 0), ("spread", 0), ("give", 3), ("sum", 1), ("spread", 1), ("grid", 3), ("pair", 3),
    ("sum", 2), ("spread", 2), ("tables", 0), ("sum", 3), ("spread", 3), ("join", 0), ("join", 1), ("join", 2),
)


def order_of_work(n):
    if n == 4 and len(SHARES) == 2:
        return ORDER
    work = [("tables", 0)]
    for i in range(n):
        work += [("give", i), ("grid", i), ("pair", i)]
    for i in range(n):
        work += [("sum", i), ("spread", i)]
    tiles = n // len(SHARES)
    return work + [("join", i) for i in range(tiles + (len(SHARES) > 1))]


def solution(mesh):
    return jax.shard_map(
        local,
        mesh=mesh,
        in_specs=(
            P("bl", "chan", None, None),
            P(),
            P("bl", None, None),
            P("bl", None, None),
            P("bl", None),
            P(("chan", "bl"), None),
        ),
        out_specs=P(("chan", "bl"), None, None, None),
        check_vma=False,
    )
```

```python
import functools
import math

import jax
import jax.numpy as jnp
import numpy as np
from jax import lax
from jax.experimental import pallas as pl
from jax.experimental.pallas import tpu as pltpu
from jax.sharding import PartitionSpec as P


UNIT = 16
SHARES = (1, 1)
DIRECT = (True, True, True, True)
PER = 8
RADIX = 4
LANES = 128


def piece_channels(ch_dev):
    units = ch_dev // UNIT
    ends = [round(units * sum(SHARES[: i + 1]) / sum(SHARES)) for i in range(len(SHARES))]
    return [(b - a) * UNIT for a, b in zip([0] + ends[:-1], ends)]


def after(x, *before):
    return lax.optimization_barrier((x,) + before)[0]


def xor_pairs(n, bit):
    return [(i, i ^ bit) for i in range(n)]


def grid_kernel(inner, owned, n_bl, off, flip, depth, lists_ref, vis, ker, out_ref):
    n_chan, rows = out_ref.shape[1:3]
    per = math.gcd(PER, n_chan)
    blocks = n_chan // per

    def step(g, _):
        half = g // blocks
        owner = lists_ref[2 * depth + 1, 0] ^ jnp.where(half == 0, 2, 0) ^ flip
        for i in range(per):
            chan = (g % blocks) * per + i
            tile = (chan * n_bl + owner) * owned + inner
            count = lists_ref[2 * depth, tile]
            lhs = [vis[lists_ref[k, tile], pl.ds(off, rows)] for k in range(depth)]
            lhs = [jnp.where(k < count, v, jnp.zeros_like(v)) for k, v in enumerate(lhs)]
            rhs = [ker[lists_ref[depth + k, tile]] for k in range(depth)]
            acc = jnp.dot(
                jnp.concatenate(lhs, axis=1), jnp.concatenate(rhs, axis=0), preferred_element_type=jnp.float32
            )
            out_ref[half, chan] = acc.astype(jnp.bfloat16)
        return 0

    lax.fori_loop(0, 2 * blocks, step, 0)


def grid_call(lists, vis, ker, inner, off, ch, n_chan, n_bl, owned, flip):
    vmem = pl.BlockSpec(memory_space=pltpu.VMEM)
    smem = pl.BlockSpec(memory_space=pltpu.SMEM)
    return pl.pallas_call(
        functools.partial(grid_kernel, inner, owned, n_bl, 2 * off, flip, (lists.shape[0] - 2) // 2),
        in_specs=[smem] + [vmem] * 2,
        out_specs=vmem,
        out_shape=jax.ShapeDtypeStruct((2, n_chan, 2 * ch, ker.shape[2]), jnp.bfloat16),
        compiler_params=pltpu.CompilerParams(vmem_limit_bytes=4 << 20),
    )(lists, vis, ker)


def pair_up(a, b):
    return (a.astype(jnp.float32) + b.astype(jnp.float32)).astype(jnp.bfloat16)


def sum_all(*parts):
    total = parts[0].astype(jnp.float32)
    for part in parts[1:]:
        total = total + part.astype(jnp.float32)
    return total.astype(jnp.bfloat16)


def sum_kernel(me_ref, keep_ref, near_ref, far_ref, *outs):
    for r, out in enumerate(outs):
        chan = me_ref[1] ^ r
        out[...] = sum_all(keep_ref[0, chan], near_ref[0, chan], far_ref[chan])


def sum_call(me, keep, near, far):
    _, n_chan, rows, cells = keep.shape
    half = pl.BlockSpec((1, n_chan, rows, cells), lambda i, *_: (1, 0, 0, 0))
    return pl.pallas_call(
        sum_kernel,
        grid_spec=pltpu.PrefetchScalarGridSpec(
            num_scalar_prefetch=1,
            grid=(1,),
            in_specs=[half, half, pl.BlockSpec((n_chan, rows, cells), lambda i, *_: (0, 0, 0))],
            out_specs=[pl.BlockSpec((rows, cells), lambda i, *_: (0, 0))] * n_chan,
        ),
        out_shape=[jax.ShapeDtypeStruct((rows, cells), jnp.bfloat16)] * n_chan,
        compiler_params=pltpu.CompilerParams(dimension_semantics=("arbitrary",), vmem_limit_bytes=12 << 20),
    )(me, keep, near, far)


def angle_tables(n_chan, ch_dev):
    nchan = n_chan * ch_dev
    delay = np.arange(nchan // RADIX, dtype=np.int64)
    start = np.arange(n_chan, dtype=np.int64)[:, None] * ch_dev
    inside = np.arange(ch_dev, dtype=np.int64).reshape(ch_dev // RADIX, RADIX).T[:, :, None]
    turn = lambda c: 2.0 * np.pi * (c * delay % nchan) / nchan
    return [jnp.asarray(f(turn(c)).astype(np.float32)) for c in (start, inside) for f in (np.cos, np.sin)]


def table_kernel(places, uc_ref, us_ref, vc_ref, vs_ref, *rest):
    n = len(places)
    outs, scratch = rest[:n], rest[n:]
    n_src = uc_ref.shape[0]
    for j, (off, ch) in enumerate(places):
        q = ch // RADIX
        cos, sin = scratch[2 * j], scratch[2 * j + 1]
        for m in range(RADIX):
            vc = vc_ref[m, pl.ds(off // RADIX, q), :]
            vs = vs_ref[m, pl.ds(off // RADIX, q), :]
            for r in range(n_src):
                uc = uc_ref[pl.ds(r, 1), :]
                us = us_ref[pl.ds(r, 1), :]
                cos[pl.ds(r * q, q), :] = uc * vc - us * vs
                sin[pl.ds(r * q, q), :] = us * vc + uc * vs
            k = n_src * q
            c = cos[...]
            s = sin[...]
            outs[j][0, m, pl.ds(0, k), pl.ds(0, LANES)] = c.astype(jnp.bfloat16)
            outs[j][0, m, pl.ds(0, k), pl.ds(LANES, LANES)] = (-s).astype(jnp.bfloat16)
            outs[j][0, m, pl.ds(k, k), pl.ds(0, LANES)] = s.astype(jnp.bfloat16)
            outs[j][0, m, pl.ds(k, k), pl.ds(LANES, LANES)] = c.astype(jnp.bfloat16)


def table_call(gate, sizes, n_chan, ch_dev):
    tables = angle_tables(n_chan, ch_dev)
    tables[0] = after(tables[0], gate)
    steps = tables[0].shape[-1] // LANES
    places, off = [], 0
    for ch in sizes:
        places.append((off, ch))
        off += ch
    spec = lambda t: pl.BlockSpec(t.shape[:-1] + (LANES,), lambda d, *_: (0,) * (t.ndim - 1) + (d,))
    return pl.pallas_call(
        functools.partial(table_kernel, places),
        grid=(steps,),
        in_specs=[spec(t) for t in tables],
        out_specs=[
            pl.BlockSpec((1, RADIX, 2 * n_chan * ch // RADIX, 2 * LANES), lambda d: (d, 0, 0, 0)) for ch in sizes
        ],
        scratch_shapes=[
            pltpu.VMEM((n_chan * ch // RADIX, LANES), jnp.float32) for ch in sizes for _ in range(2)
        ],
        out_shape=[
            jax.ShapeDtypeStruct((steps, RADIX, 2 * n_chan * ch // RADIX, 2 * LANES), jnp.bfloat16)
            for ch in sizes
        ],
        compiler_params=pltpu.CompilerParams(dimension_semantics=("arbitrary",), vmem_limit_bytes=12 << 20),
        name="tables",
    )(*tables)


def turn_kernel(counts, has_acc, inner, scale, me_ref, *refs):
    final = inner is not None
    rest = list(refs)
    gs = [[rest.pop(0) for _ in range(c)] for c in counts]
    ts = [rest.pop(0) for _ in counts]
    acc_ref = rest.pop(0) if has_acc else None
    if final:
        mask_ref, _, out_hbm, turned, stage, bins, sems = rest
    else:
        out_ref, turned, stage = rest
    d = pl.program_id(0)
    steps = pl.num_programs(0)

    @pl.when(d == 0)
    def _():
        at = 0
        for g in gs:
            if len(g) == 1:
                n_src, rows, _ = g[0].shape
            else:
                n_src, rows = len(g), g[0].shape[0]
            for r in range(n_src):
                for h in range(stage.shape[0]):
                    lanes = pl.ds(h * LANES, LANES)
                    if len(g) == 1:
                        stage[h, pl.ds(r * rows, rows), :] = g[0][r, :, lanes].astype(jnp.float32)
                    else:
                        start = pl.multiple_of((me_ref[1] ^ r) * rows, 8)
                        stage[h, pl.ds(start, rows), :] = g[r][:, lanes].astype(jnp.float32)
            k = n_src * rows // (2 * RADIX)
            for m in range(RADIX):
                for h in range(stage.shape[0]):
                    parts = [
                        stage[h, pl.ds(2 * m + p, k, stride=2 * RADIX), :].astype(jnp.bfloat16) for p in range(2)
                    ]
                    turned[m, pl.ds(h * LANES, LANES), pl.ds(at, 2 * k)] = jnp.concatenate(parts, axis=0).T
            at += 2 * k

    sums = []
    for m in range(RADIX):
        at = 0
        total = None
        for t in ts:
            k = t.shape[2]
            part = jnp.dot(turned[m, :, pl.ds(at, k)], t[0, m], preferred_element_type=jnp.float32)
            total = part if total is None else total + part
            at += k
        if has_acc:
            total = total + acc_ref[0, m]
        sums.append(total)
    if not final:
        for m in range(RADIX):
            out_ref[0, m] = sums[m]
        return

    def copies(step):
        slot = step % 2
        width = steps * LANES
        return [
            pltpu.make_async_copy(
                bins.at[slot, j],
                out_hbm.at[inner, :, :, pl.ds(pl.multiple_of(j * width + step * LANES, LANES), LANES)],
                sems.at[slot, j],
            )
            for j in range(RADIX)
        ]

    @pl.when(d >= 2)
    def _():
        for c in copies(d - 2):
            c.wait()

    re = [s[:, :LANES] for s in sums]
    im = [s[:, LANES:] for s in sums]
    e0r, e0i, e1r, e1i = re[0] + re[2], im[0] + im[2], re[0] - re[2], im[0] - im[2]
    o0r, o0i, o1r, o1i = re[1] + re[3], im[1] + im[3], re[1] - re[3], im[1] - im[3]
    joined = (
        (e0r + o0r, e0i + o0i),
        (e1r + o1i, e1i - o1r),
        (e0r - o0r, e0i - o0i),
        (e1r - o1i, e1i + o1r),
    )
    slot = d % 2
    for j, parts in enumerate(joined):
        at = pl.ds(pl.multiple_of((j * steps + d) * LANES, LANES), LANES)
        keep = mask_ref[pl.ds(inner, 1), at].astype(jnp.float32) * scale
        for p, value in enumerate(parts):
            bins[slot, j, p] = value * keep
    for c in copies(d):
        c.start()

    @pl.when(d == steps - 1)
    def _():
        for back in range(min(2, out_hbm.shape[3] // (RADIX * LANES)) - 1, -1, -1):
            for c in copies(d - back):
                c.wait()


def turn_call(me, gs, ts, acc, mask, out, inner):
    cells = gs[0][0].shape[-1]
    steps = ts[0].shape[0]
    final = inner is not None
    has_acc = acc is not None
    k = sum(t.shape[2] for t in ts)
    whole = lambda a: pl.BlockSpec(a.shape, lambda d, *_: (0,) * a.ndim, pipeline_mode=pl.Buffered(1))
    acc_spec = pl.BlockSpec((1, RADIX, cells, 2 * LANES), lambda d, *_: (d, 0, 0, 0))
    ins = [a for g in gs for a in g]
    specs = [whole(a) for a in ins]
    ins += ts
    specs += [pl.BlockSpec((1,) + t.shape[1:], lambda d, *_: (d, 0, 0, 0)) for t in ts]
    if has_acc:
        ins.append(acc)
        specs.append(acc_spec)
    scratch = [
        pltpu.VMEM((RADIX, cells, k), jnp.bfloat16),
        pltpu.VMEM((cells // LANES, max(sum(a.size for a in g) for g in gs) // cells, LANES), jnp.float32),
    ]
    if final:
        alias = {len(ins) + 2: 0}
        ins += [mask, out]
        specs += [whole(mask), pl.BlockSpec(memory_space=pltpu.HBM)]
        out_spec = pl.BlockSpec(memory_space=pltpu.HBM)
        out_shape = jax.ShapeDtypeStruct(out.shape, out.dtype)
        scratch += [
            pltpu.VMEM((2, RADIX, 2, cells, LANES), jnp.float32),
            pltpu.SemaphoreType.DMA((2, RADIX)),
        ]
    else:
        alias = {}
        out_spec = acc_spec
        out_shape = jax.ShapeDtypeStruct((steps, RADIX, cells, 2 * LANES), jnp.float32)
    nchan = steps * RADIX * LANES
    return pl.pallas_call(
        functools.partial(turn_kernel, [len(g) for g in gs], has_acc, inner, 1.0 / math.sqrt(nchan)),
        grid_spec=pltpu.PrefetchScalarGridSpec(
            num_scalar_prefetch=1,
            grid=(steps,),
            in_specs=specs,
            out_specs=out_spec,
            scratch_shapes=scratch,
        ),
        out_shape=out_shape,
        input_output_aliases=alias,
        compiler_params=pltpu.CompilerParams(dimension_semantics=("arbitrary",), vmem_limit_bytes=14 << 20),
    )(me, *ins)


def empty_kernel(out_ref):
    pass


def empty(shape):
    return pl.pallas_call(
        empty_kernel,
        out_specs=pl.BlockSpec(memory_space=pltpu.HBM),
        out_shape=jax.ShapeDtypeStruct(shape, jnp.float32),
        compiler_params=pltpu.CompilerParams(vmem_limit_bytes=1 << 20),
        name="empty",
    )()


def local(visibilities, kernels, block_ids, kernel_ids, tile_counts, wedge_mask):
    n_chan = lax.axis_size("chan")
    n_bl = lax.axis_size("bl")
    nblocks, ch_dev, _, block_len = visibilities.shape
    cells = kernels.shape[2]
    owned = wedge_mask.shape[0]
    nchan = ch_dev * n_chan
    vis = visibilities.reshape(nblocks, ch_dev * 2, block_len)
    me = jnp.stack([lax.axis_index("bl"), lax.axis_index("chan")]).astype(jnp.int32)
    place = jnp.full((1, tile_counts.shape[1]), me[0], jnp.int32)
    lists = jnp.concatenate([block_ids[0].T, kernel_ids[0].T, tile_counts, place], axis=0)
    sizes = piece_channels(ch_dev)
    n = len(sizes)
    starts = [sum(sizes[:j]) for j in range(n)]
    blocks = []
    for inner in range(owned):
        blocks += [(inner, j) for j in (range(n) if inner < owned - 1 else range(n - 1, -1, -1))]
    keep, near, sent, far, total, arrived = {}, {}, {}, {}, {}, {}
    tables = out = acc = None
    gate = me

    for what, i in order_of_work(len(blocks)):
        if what in ("give", "grid"):
            inner, j = blocks[i]
            part = grid_call(
                after(lists, gate), vis, kernels,
                inner, starts[j], sizes[j], n_chan, n_bl, owned, int(what == "give"),
            )
            gate = part
            if what == "grid":
                keep[i] = part
            else:
                near[i] = lax.ppermute(part, "bl", xor_pairs(n_bl, 1))
        elif what == "tables":
            tables = table_call(gate, sizes, n_chan, ch_dev)
            gate = tables[0]
        elif what == "pair":
            gate = sent[i] = pair_up(after(keep[i], gate)[0], near[i][0])
            far[i] = lax.ppermute(sent[i], "bl", xor_pairs(n_bl, 2))
        elif what == "sum":
            if DIRECT[i % len(DIRECT)]:
                total[i] = sum_call(me, after(keep[i], gate), near[i], far[i])
                gate = total[i][0]
            else:
                gate = total[i] = sum_all(after(keep[i], gate)[1], near[i][1], far[i])
        elif what == "spread":
            if DIRECT[i % len(DIRECT)]:
                arrived[blocks[i]] = list(total[i])
                for r in range(1, n_chan):
                    arrived[blocks[i]][r] = lax.ppermute(total[i][r], "chan", xor_pairs(n_chan, r))
            else:
                arrived[blocks[i]] = [lax.all_to_all(total[i], "chan", 0, 0, tiled=True)]
        elif what == "join":
            if out is None:
                out = empty((owned, 2, cells, nchan))
            if i < owned - 1:
                got, last = [(i, j) for j in range(n)], True
            elif n > 1 and i == owned - 1:
                got, last = blocks[-n:-1], False
            else:
                got, last = blocks[-1:], True
            gs = [arrived[key] for key in got]
            gs[0] = [after(gs[0][0], gate)] + gs[0][1:]
            ts = [tables[j] for _, j in got]
            if last:
                gate = out = turn_call(me, gs, ts, acc, wedge_mask, out, got[0][0])
            else:
                gate = acc = turn_call(me, gs, ts, None, None, None, None)
    return out


ORDER = (
    ("give", 0), ("grid", 0), ("pair", 0), ("give", 1), ("grid", 1), ("give", 2), ("pair", 1), ("grid", 2),
    ("pair", 2), ("sum", 0), ("spread", 0), ("give", 3), ("sum", 1), ("spread", 1), ("grid", 3), ("pair", 3),
    ("sum", 2), ("spread", 2), ("tables", 0), ("sum", 3), ("spread", 3), ("join", 0), ("join", 1), ("join", 2),
)


def order_of_work(n):
    if n == 4 and len(SHARES) == 2:
        return ORDER
    work = [("tables", 0)]
    for i in range(n):
        work += [("give", i), ("grid", i), ("pair", i)]
    for i in range(n):
        work += [("sum", i), ("spread", i)]
    tiles = n // len(SHARES)
    return work + [("join", i) for i in range(tiles + (len(SHARES) > 1))]


def solution(mesh):
    return jax.shard_map(
        local,
        mesh=mesh,
        in_specs=(
            P("bl", "chan", None, None),
            P(),
            P("bl", None, None),
            P("bl", None, None),
            P("bl", None),
            P(("chan", "bl"), None),
        ),
        out_specs=P(("chan", "bl"), None, None, None),
        check_vma=False,
    )
```
